32 devices in a mesh: ctx: 16 (over z, x, core), tp: 2 (over y).
Axes of the slice: x: 2, y: 2, z: 4, core: 2. Of those that a mesh axis runs over, the one named last changes fastest.
Arguments:
- hidden: bfloat16 [2048, 7168], P('ctx', 'tp'), may hold values from -500 to 500
- embed: bfloat16 [2048, 7168], P('ctx', 'tp'), may hold values from -500 to 500
- gain_hidden: float32 [7168], P('tp'), may hold values from 0.1 to 1.9
- gain_embed: float32 [7168], P('tp'), may hold values from 0.1 to 1.9
- proj_hidden: bfloat16 [7168, 576], P('tp'), may hold values from -0.0625 to 0.0625
- proj_embed: bfloat16 [7168, 576], P('tp'), may hold values from -0.0625 to 0.0625
- gain_latent: float32 [512], replicated, may hold values from 0.1 to 1.9
- key_up: bfloat16 [512, 8192], P(None, 'tp'), may hold values from -0.25 to 0.25
- value_up: bfloat16 [512, 8192], P(None, 'tp'), may hold values from -0.25 to 0.25
- queries: bfloat16 [2048, 12288], P('ctx', 'tp'), may hold values from -60 to 60
- grad_out: bfloat16 [2048, 8192], P('ctx', 'tp'), may hold values from -6 to 6
Outputs:
- attended: bfloat16 [2048, 8192], P('ctx', 'tp')
- grad_queries: bfloat16 [2048, 12288], P('ctx', 'tp')
- grad_hidden: bfloat16 [2048, 7168], P('ctx', 'tp')
- grad_embed: bfloat16 [2048, 7168], P('ctx', 'tp')
The draws below stay inside these ranges and needn't reach their ends.
All inputs are finite; a program needn't handle non-finite values.
Results may differ from the reference program's by a relative error of at most 0.019.
The reference program's roundings to bfloat16 on the way count: a program that leaves them out, or rounds other values in their place, can miss the bound.
Values may be sent and summed in bfloat16 or wider, within the bound.
A program may use at most 192 MiB of HBM per device.

```python
import math
import jax
import jax.numpy as jnp
from jax import lax

D = 7168
LAT = 512
ROPE = 64
NOPE = 128
VDIM = 128
H = 64
SEQ = 2048
N_CTX = 16


def feature_values(key, row_count, column_count):
    splits = jax.random.split(key, 3)
    column_ramp = jnp.arange(column_count, dtype=jnp.float32) / column_count
    base_values = jnp.clip(jax.random.normal(splits[0], (row_count, column_count), jnp.float32), -6.0, 6.0)
    row_scale = jnp.exp(jax.random.uniform(splits[1], (row_count, 1), jnp.float32, 0.0, math.log(10.0)))
    column_scale = 3.0 ** column_ramp * jnp.exp(jax.random.uniform(splits[2], (column_count,), jnp.float32, 0.0, math.log(3.4)))
    return base_values * row_scale * column_scale / 3.0


def draw_hidden(key, part):
    return feature_values(jax.random.fold_in(key, 101), SEQ, D).astype(jnp.bfloat16)


def draw_embed(key, part):
    return feature_values(jax.random.fold_in(key, 202), SEQ, D).astype(jnp.bfloat16)


def draw_queries(key, part):
    splits = jax.random.split(jax.random.fold_in(key, 303), 1)
    array_shape = (SEQ, H * (NOPE + ROPE))
    values = 2.5 * jnp.clip(jax.random.normal(splits[0], array_shape, jnp.float32), -6.0, 6.0)
    return values.astype(jnp.bfloat16)


def shard_levels(own_key, extent, cuts, low, top_value):
    def one(axis_at, blocks):
        heights = jax.random.uniform(jax.random.fold_in(jax.random.fold_in(own_key, 6), axis_at), (blocks,), jnp.float32, low / len(cuts), top_value / len(cuts))
        return jnp.repeat(jnp.exp(heights), extent[axis_at] // blocks).reshape((-1,) + (1,) * (len(extent) - axis_at - 1))

    level = one(*cuts[0])
    for cut in cuts[1:]:
        level = level * one(*cut)
    return level


def centred(key, extent, spread, limit, cuts=(), kind=jnp.bfloat16):
    values = jax.random.normal(key, extent, jnp.float32) * spread
    if len(cuts) > 0:
        values = shard_levels(key, extent, cuts, -0.22, 0.18) * values
    return jnp.clip(values, min=-limit, max=limit).astype(kind)


def setup_inputs(seed: int = 0) -> dict:
    seeds = jax.random.split(jax.random.key(seed), 12)
    return {
        "hidden": draw_hidden(jax.random.fold_in(seeds[11], 71), 0),
        "embed": draw_embed(jax.random.fold_in(seeds[11], 71), 0),
        "gain_hidden": jnp.clip(1.0 + 0.18 * jax.random.normal(seeds[2], (D,), jnp.float32), 0.1, 1.9),
        "gain_embed": jnp.clip(1.0 + 0.18 * jax.random.normal(seeds[3], (D,), jnp.float32), 0.1, 1.9),
        "proj_hidden": centred(seeds[4], (D, LAT + ROPE), D ** -0.5, 0.0625, ((0, 2),)),
        "proj_embed": centred(seeds[5], (D, LAT + ROPE), D ** -0.5, 0.0625, ((0, 2),)),
        "gain_latent": jnp.clip(1.0 + 0.18 * jax.random.normal(seeds[6], (LAT,), jnp.float32), 0.1, 1.9),
        "key_up": centred(seeds[7], (LAT, H * NOPE), LAT ** -0.5, 0.25, ((1, 2),)),
        "value_up": centred(seeds[8], (LAT, H * VDIM), LAT ** -0.5, 0.25, ((1, 2),)),
        "queries": draw_queries(jax.random.fold_in(seeds[11], 71), 0),
        "grad_out": centred(seeds[10], (SEQ, H * VDIM), 1.0, 6.0, ((0, 16), (1, 2))),
    }


EPSILON = 1e-06
ROTARY_BASE = 10000.0

def rounded(values):
    return lax.optimization_barrier(values.astype(jnp.bfloat16)).astype(jnp.float32)

def rotation(positions):
    pair_count = ROPE // 2
    frequency = ROTARY_BASE ** (-jnp.arange(pair_count, dtype=jnp.float32) / pair_count)
    angles = positions.astype(jnp.float32)[:, None] * frequency[None, :]
    return (jnp.cos(angles), jnp.sin(angles))

def rotate_pairs(values, cos_table, sin_table):
    pair_count = ROPE // 2
    first_half = values[..., :pair_count]
    second_half = values[..., pair_count:]
    return jnp.concatenate([first_half * cos_table - second_half * sin_table, first_half * sin_table + second_half * cos_table], axis=-1)

def unrotate(values, cos_table, sin_table):
    pair_count = ROPE // 2
    first_half = values[..., :pair_count]
    second_half = values[..., pair_count:]
    return jnp.concatenate([first_half * cos_table + second_half * sin_table, second_half * cos_table - first_half * sin_table], axis=-1)

def to_positions(values):
    half_rows = values.shape[0] // (2 * N_CTX)
    trailing = values.shape[1:]
    shaped = values.reshape((N_CTX, 2, half_rows) + trailing)
    early_rows = shaped[:, 0].reshape((N_CTX * half_rows,) + trailing)
    late_rows = shaped[::-1, 1].reshape((N_CTX * half_rows,) + trailing)
    return jnp.concatenate([early_rows, late_rows], axis=0)

def to_rows(values):
    half_rows = values.shape[0] // (2 * N_CTX)
    trailing = values.shape[1:]
    early_rows = values[:N_CTX * half_rows].reshape((N_CTX, half_rows) + trailing)
    late_rows = values[N_CTX * half_rows:].reshape((N_CTX, half_rows) + trailing)[::-1]
    return jnp.stack([early_rows, late_rows], axis=1).reshape((2 * N_CTX * half_rows,) + trailing)

def reference(hidden, embed, gain_hidden, gain_embed, proj_hidden, proj_embed, gain_latent, key_up, value_up, queries, grad_out):
    seq_total = hidden.shape[0]
    head_count = key_up.shape[1] // NOPE
    score_scale = (NOPE + ROPE) ** (-0.5)
    key_block = max(256, seq_total // 16)
    hidden_pos = to_positions(hidden)
    embed_pos = to_positions(embed)
    next_embed = jnp.concatenate([embed_pos[1:], jnp.zeros((1, embed.shape[1]), embed.dtype)], axis=0)
    hidden_wide = hidden_pos.astype(jnp.float32)
    next_wide = next_embed.astype(jnp.float32)
    inv_hidden = lax.rsqrt(lax.optimization_barrier(jnp.sum(hidden_wide * hidden_wide, axis=1, keepdims=True)) / D + EPSILON)
    inv_next = lax.rsqrt(lax.optimization_barrier(jnp.sum(next_wide * next_wide, axis=1, keepdims=True)) / D + EPSILON)
    scaled_hidden = (hidden_wide * gain_hidden).astype(jnp.bfloat16)
    scaled_next = (next_wide * gain_embed).astype(jnp.bfloat16)
    part_hidden = jnp.dot(scaled_hidden, proj_hidden, preferred_element_type=jnp.float32)
    part_next = jnp.dot(scaled_next, proj_embed, preferred_element_type=jnp.float32)
    latent = inv_hidden * part_hidden + inv_next * part_next
    leading = latent[:, :LAT]
    inv_latent = lax.rsqrt(lax.optimization_barrier(jnp.mean(leading * leading, axis=1, keepdims=True)) + EPSILON)
    key_latent = (leading * inv_latent * gain_latent).astype(jnp.bfloat16)
    positions = jnp.arange(seq_total, dtype=jnp.int32)
    cos_table, sin_table = rotation(positions)
    key_rope = rotate_pairs(latent[:, LAT:], cos_table, sin_table).astype(jnp.bfloat16)
    key_table = jnp.concatenate([key_latent, key_rope], axis=1)
    query_heads = to_positions(queries).reshape(seq_total, head_count, NOPE + ROPE).astype(jnp.float32)
    query_rot = rotate_pairs(query_heads[..., NOPE:], cos_table[:, None], sin_table[:, None]).astype(jnp.bfloat16)
    key_up_heads = key_up.reshape(LAT, head_count, NOPE).astype(jnp.float32)
    value_up_heads = value_up.reshape(LAT, head_count, VDIM).astype(jnp.float32)
    query_latent = jnp.einsum('shn,lhn->shl', query_heads[..., :NOPE], key_up_heads).astype(jnp.bfloat16)
    query_full = jnp.swapaxes(jnp.concatenate([query_latent, query_rot], axis=2), 0, 1)
    grad_heads = to_positions(grad_out).reshape(seq_total, head_count, VDIM).astype(jnp.float32)
    grad_latent = jnp.swapaxes(jnp.einsum('shv,lhv->shl', grad_heads, value_up_heads).astype(jnp.bfloat16), 0, 1)
    grad_keys = jnp.zeros((seq_total, LAT + ROPE), jnp.float32)
    out_blocks = []
    grad_query_blocks = []
    for block_index in range(seq_total // key_block):
        first_row = block_index * key_block
        last_row = first_row + key_block
        key_slab = key_table[:last_row].astype(jnp.float32)
        allowed = jnp.arange(last_row, dtype=jnp.int32)[None, :] <= jnp.arange(first_row, last_row, dtype=jnp.int32)[:, None]

        def per_head(state_keys, inputs):
            query_block, grad_block = inputs
            query_wide = query_block.astype(jnp.float32)
            grad_wide = grad_block.astype(jnp.float32)
            scores = jnp.dot(query_wide, key_slab.T, preferred_element_type=jnp.float32) * score_scale
            scores = jnp.where(allowed, scores, -jnp.inf)
            weights = jnp.exp(scores - lax.optimization_barrier(jnp.max(scores, axis=1, keepdims=True)))
            prob_wide = rounded(weights / lax.optimization_barrier(jnp.sum(weights, axis=1, keepdims=True)))
            out_latent = jnp.dot(prob_wide, key_slab[:, :LAT], preferred_element_type=jnp.float32)
            delta_rows = lax.optimization_barrier(jnp.sum(grad_wide * out_latent, axis=1, keepdims=True))
            grad_prob = jnp.dot(grad_wide, key_slab[:, :LAT].T, preferred_element_type=jnp.float32)
            grad_score = rounded(prob_wide * (grad_prob - delta_rows) * score_scale)
            grad_query = jnp.dot(grad_score, key_slab, preferred_element_type=jnp.float32)
            grad_lead = jnp.dot(grad_score.T, query_wide[:, :LAT], preferred_element_type=jnp.float32) + jnp.dot(prob_wide.T, grad_wide, preferred_element_type=jnp.float32)
            grad_tail = jnp.dot(grad_score.T, query_wide[:, LAT:], preferred_element_type=jnp.float32)
            return (state_keys + jnp.concatenate([grad_lead, grad_tail], axis=1), (out_latent.astype(jnp.bfloat16), grad_query))
        block_keys, (out_heads, grad_heads_q) = lax.scan(per_head, jnp.zeros((last_row, LAT + ROPE), jnp.float32), (query_full[:, first_row:last_row], grad_latent[:, first_row:last_row]))
        grad_keys = grad_keys + jnp.pad(block_keys, ((0, seq_total - last_row), (0, 0)))
        out_blocks.append(out_heads)
        grad_query_blocks.append(grad_heads_q)
    out_all = jnp.concatenate(out_blocks, axis=1)
    grad_query_all = jnp.concatenate(grad_query_blocks, axis=1)
    attended = jnp.einsum('hsl,lhv->shv', out_all.astype(jnp.float32), value_up_heads).astype(jnp.bfloat16).reshape(seq_total, head_count * VDIM)
    grad_lead_q = rounded(grad_query_all[..., :LAT])
    grad_nope = jnp.einsum('hsl,lhn->shn', grad_lead_q, key_up_heads)
    grad_rope = unrotate(jnp.swapaxes(grad_query_all[..., LAT:], 0, 1), cos_table[:, None], sin_table[:, None])
    grad_queries = jnp.concatenate([grad_nope, grad_rope], axis=2).astype(jnp.bfloat16).reshape(seq_total, head_count * (NOPE + ROPE))
    grad_rope_key = unrotate(grad_keys[:, LAT:], cos_table, sin_table)
    gained = gain_latent * grad_keys[:, :LAT]
    grad_leading = inv_latent * gained - inv_latent ** 3 * leading * lax.optimization_barrier(jnp.sum(gained * leading, axis=1, keepdims=True)) / LAT
    grad_lat = jnp.concatenate([grad_leading, grad_rope_key], axis=1)
    part_grad_hidden = (inv_hidden * grad_lat).astype(jnp.bfloat16)
    part_grad_next = (inv_next * grad_lat).astype(jnp.bfloat16)
    coef_hidden = lax.optimization_barrier(jnp.sum(grad_lat * part_hidden, axis=1, keepdims=True)) * inv_hidden ** 3 / D
    coef_next = lax.optimization_barrier(jnp.sum(grad_lat * part_next, axis=1, keepdims=True)) * inv_next ** 3 / D
    grad_hidden = (gain_hidden * jnp.dot(part_grad_hidden, proj_hidden.T, preferred_element_type=jnp.float32) - coef_hidden * hidden_wide).astype(jnp.bfloat16)
    grad_next = gain_embed * jnp.dot(part_grad_next, proj_embed.T, preferred_element_type=jnp.float32) - coef_next * next_wide
    grad_embed = jnp.concatenate([jnp.zeros((1, grad_next.shape[1]), jnp.float32), grad_next[:-1]], axis=0).astype(jnp.bfloat16)
    return (to_rows(attended), to_rows(grad_queries), to_rows(grad_hidden), to_rows(grad_embed))
```

```python
import functools

import jax
import jax.numpy as jnp
from jax import lax
from jax.experimental import pallas as pl
from jax.experimental.pallas import tpu as pltpu
from jax.sharding import PartitionSpec as P

D = 7168
LAT = 512
ROPE = 64
NOPE = 128
VDIM = 128


EPSILON = 1e-06
ROTARY_BASE = 10000.0


def with_halo(x, sides, width):
    for axis, dim in sides:
        size, length = (lax.axis_size(axis), x.shape[dim])
        up = [(i, (i + 1) % size) for i in range(size - 1)]
        down = [(j, i) for i, j in up]
        last = lax.slice_in_dim(x, length - width, length, axis=dim)
        first = lax.slice_in_dim(x, 0, width, axis=dim)
        before = lax.ppermute(last, axis, up)
        after = lax.ppermute(first, axis, down)
        x = jnp.concatenate([before, x, after], axis=dim)
    return x


def rotation(positions):
    pair_count = ROPE // 2
    frequency = ROTARY_BASE ** (-jnp.arange(pair_count, dtype=jnp.float32) / pair_count)
    angles = positions.astype(jnp.float32)[:, None] * frequency[None, :]
    return (jnp.cos(angles), jnp.sin(angles))


def rotate_pairs(values, cos_table, sin_table):
    pair_count = ROPE // 2
    first_half = values[..., :pair_count]
    second_half = values[..., pair_count:]
    return jnp.concatenate(
        [
            first_half * cos_table - second_half * sin_table,
            first_half * sin_table + second_half * cos_table,
        ],
        axis=-1,
    )


def unrotate(values, cos_table, sin_table):
    pair_count = ROPE // 2
    first_half = values[..., :pair_count]
    second_half = values[..., pair_count:]
    return jnp.concatenate(
        [
            first_half * cos_table + second_half * sin_table,
            second_half * cos_table - first_half * sin_table,
        ],
        axis=-1,
    )


def local_positions(tokens, ctx_index, groups):
    half_rows = tokens // 2
    offsets = jnp.arange(tokens, dtype=jnp.int32)
    early_pos = ctx_index * half_rows + offsets
    late_pos = (2 * groups - 1 - ctx_index) * half_rows + offsets - half_rows
    return jnp.where(offsets < half_rows, early_pos, late_pos)


def finish_latent(part_hidden, part_next, squares, gain_latent, positions):
    inverse = lax.rsqrt(squares / D + EPSILON)
    latent = inverse[:, 0:1] * part_hidden + inverse[:, 1:2] * part_next
    leading = latent[:, :LAT]
    inv_latent = lax.rsqrt(jnp.mean(leading * leading, axis=1, keepdims=True) + EPSILON)
    key_latent = (leading * inv_latent * gain_latent).astype(jnp.bfloat16)
    cos_table, sin_table = rotation(positions)
    key_rope = rotate_pairs(latent[:, LAT:], cos_table, sin_table).astype(jnp.bfloat16)
    return (key_latent, key_rope, latent, inverse, inv_latent)


def latent_backward(
    grad_key_latent,
    grad_key_rope,
    latent,
    inverse,
    inv_latent,
    gain_latent,
    positions,
    part_hidden,
    part_next,
):
    cos_table, sin_table = rotation(positions)
    grad_rope = unrotate(grad_key_rope, cos_table, sin_table)
    leading = latent[:, :LAT]
    gained = gain_latent * grad_key_latent
    grad_leading = (
        inv_latent * gained
        - inv_latent**3 * leading * jnp.sum(gained * leading, axis=1, keepdims=True) / LAT
    )
    grad_latent = jnp.concatenate([grad_leading, grad_rope], axis=1)
    part_grad_hidden = (inverse[:, 0:1] * grad_latent).astype(jnp.bfloat16)
    part_grad_next = (inverse[:, 1:2] * grad_latent).astype(jnp.bfloat16)
    inv_sums = jnp.concatenate(
        [
            jnp.sum(grad_latent * part_hidden, axis=1, keepdims=True),
            jnp.sum(grad_latent * part_next, axis=1, keepdims=True),
        ],
        axis=1,
    )
    coefficient = inv_sums * inverse**3 / D
    return (part_grad_hidden, part_grad_next, coefficient)


UNROLL = 9


def group_size(head_count):
    for size in (8, 4, 2, 1):
        if head_count % size == 0:
            return size


NT = (((1,), (1,)), ((), ()))
LOG2E = 1.4426950408889634


def nn_dot(a, b):
    return jnp.dot(a, b, preferred_element_type=jnp.float32)


def nt_dot(a, b):
    return lax.dot_general(a, b, NT, preferred_element_type=jnp.float32)


def identity(size):
    row = lax.broadcasted_iota(jnp.int32, (size, size), 0)
    col = lax.broadcasted_iota(jnp.int32, (size, size), 1)
    return jnp.where(row == col, 1.0, 0.0).astype(jnp.bfloat16)


def rope_picker():
    half = ROPE // 2
    row = lax.broadcasted_iota(jnp.int32, (2 * ROPE, ROPE), 0)
    col = lax.broadcasted_iota(jnp.int32, (2 * ROPE, ROPE), 1)
    plain = (row == col).astype(jnp.float32)
    swapped = (row == col + ROPE + half).astype(jnp.float32) - (
        (row == col + half) & (col >= half)
    ).astype(jnp.float32)
    return (plain + swapped).astype(jnp.bfloat16)


def pick_slots(groups):
    return [
        (2 * c + part, (part, d % 2, y, (d // 2) % 2, d // 4))
        for c in range(2 * groups)
        for y, d in [(0, c) if c < groups else (1, 2 * groups - 1 - c)]
        for part in range(2)
    ]


def attention_kernel(
    groups,
    group,
    key_block,
    score_scale,
    keys_ref,
    queries_ref,
    grad_out_ref,
    key_up_ref,
    value_up_ref,
    cos_ref,
    sin_ref,
    attended_ref,
    grad_queries_ref,
    grad_keys_ref,
    table,
    table_t,
    query_t,
    grad_t,
    weight_buf,
    dprob_buf,
    max_buf,
    out_acc,
    dquery_acc,
    dkey_acc,
    row_stat,
    eye,
):
    step = pl.program_id(0)
    ctx_index = lax.axis_index("ctx")
    tokens = queries_ref.shape[0]
    half_rows = tokens // 2
    rows = group * half_rows
    key_total = table.shape[0]
    width = LAT + ROPE
    padded = table.shape[1]
    blocks = key_total // key_block
    quarter = half_rows // 2
    pieces_of = pick_slots(groups)
    half = ROPE // 2
    chunk = eye.shape[0]

    @pl.when(step == 0)
    def _():
        eye[...] = identity(chunk)
        dkey_acc[...] = jnp.zeros_like(dkey_acc)
        query_t[...] = jnp.zeros_like(query_t)
        for piece, slot in pieces_of:
            part = keys_ref[slot]
            pad = jnp.zeros((quarter, padded - width), part.dtype)
            table[piece * quarter : (piece + 1) * quarter, :] = jnp.concatenate(
                [part, pad], axis=1
            )

        @pl.loop(0, blocks)
        def _(j):
            first = pl.multiple_of(j * key_block, key_block)
            for k in range(0, padded, 128):
                turned = nt_dot(eye[:128, :128], table[pl.ds(first, key_block), k : k + 128])
                stop = min(k + 128, width)
                table_t[j, k:stop, :] = turned[: stop - k].astype(jnp.bfloat16)

    picker = rope_picker()
    zero = jnp.zeros((half_rows, NOPE), jnp.bfloat16)

    def spread(a, b):
        return jnp.concatenate(
            [
                jnp.concatenate([a[:half_rows], zero], axis=1),
                jnp.concatenate([zero, b[:half_rows]], axis=1),
                jnp.concatenate([a[half_rows:], zero], axis=1),
                jnp.concatenate([zero, b[half_rows:]], axis=1),
            ],
            axis=0,
        )

    pair = 2 * half_rows
    head = NOPE + ROPE
    for i in range(group // 2):
        two = queries_ref[:, i * 2 * head : (i + 1) * 2 * head]
        lead = nt_dot(
            key_up_ref[:, i * 2 * NOPE : (i + 1) * 2 * NOPE],
            spread(two[:, :NOPE], two[:, head : head + NOPE]),
        ).astype(jnp.bfloat16)
        ropes = [two[:, NOPE:head], two[:, head + NOPE :]]
        rope = nt_dot(
            picker,
            jnp.concatenate([r[s] for s in (slice(0, half_rows), slice(half_rows, tokens)) for r in ropes], axis=0),
        )
        grads = nt_dot(
            value_up_ref[:, i * 2 * VDIM : (i + 1) * 2 * VDIM],
            spread(
                grad_out_ref[:, 2 * i * VDIM : (2 * i + 1) * VDIM],
                grad_out_ref[:, (2 * i + 1) * VDIM : (2 * i + 2) * VDIM],
            ),
        ).astype(jnp.bfloat16)
        to = slice(i * pair, (i + 1) * pair)
        for h in range(2):
            of = slice(h * pair, (h + 1) * pair)
            query_t[h, :LAT, to] = lead[:, of]
            query_t[h, LAT:width, to] = (
                rope[:ROPE, of] * cos_ref[h] + rope[ROPE:, of] * sin_ref[h]
            ).astype(jnp.bfloat16)
            grad_t[h, :, to] = grads[:, of]

    early_pos = ctx_index * half_rows
    late_pos = (2 * groups - 1 - ctx_index) * half_rows
    early_count = (early_pos + half_rows + key_block - 1) // key_block
    tiles = blocks + 1
    unroll = UNROLL if tiles % UNROLL == 0 else 1
    gap = lax.broadcasted_iota(jnp.int32, (key_block, rows), 1) % half_rows - (
        lax.broadcasted_iota(jnp.int32, (key_block, rows), 0)
    )
    factor = score_scale * LOG2E

    def locate(tile):
        late = (tile >= early_count).astype(jnp.int32)
        block = tile - late * early_count
        return late, block, pl.multiple_of(block * key_block, key_block)

    def over_tiles(body):
        @pl.loop(0, tiles // unroll)
        def _(trip):
            for k in range(unroll):
                body(trip * unroll + k)

    row_stat[0] = jnp.full(row_stat.shape[1:], -1e30, jnp.float32)
    row_stat[1] = jnp.zeros(row_stat.shape[1:], jnp.float32)
    row_stat[2] = jnp.zeros(row_stat.shape[1:], jnp.float32)
    out_acc[...] = jnp.zeros_like(out_acc)
    dquery_acc[...] = jnp.zeros_like(dquery_acc)

    def score_tile(tile):
        late, block, first = locate(tile)
        shift = first - jnp.where(late == 1, late_pos, early_pos)
        keys = table[pl.ds(first, key_block), :]
        scores = nn_dot(keys, query_t[late])
        scores = jnp.where(gap >= shift, scores, -1e30)
        dprob = nn_dot(keys[:, :LAT], grad_t[late])
        dprob_buf[tile] = dprob
        before = row_stat[0, late]
        top = jnp.maximum(before, jnp.max(scores, axis=0, keepdims=True))
        row_stat[0, late] = top
        max_buf[tile] = top
        weights = jnp.exp2((scores - top[:1]) * factor)
        weight_buf[tile] = weights
        keep = jnp.exp2((before - top) * factor)
        row_stat[1, late] = row_stat[1, late] * keep + jnp.sum(weights, axis=0, keepdims=True)
        row_stat[2, late] = row_stat[2, late] * keep + jnp.sum(
            weights * dprob, axis=0, keepdims=True
        )

    over_tiles(score_tile)
    for h in range(2):
        inv_sum = 1.0 / row_stat[1, h]
        row_stat[1, h] = inv_sum
        row_stat[2, h] = row_stat[2, h] * inv_sum

    def grad_tile(tile):
        late, block, first = locate(tile)
        level = jnp.exp2((max_buf[tile] - row_stat[0, late]) * factor) * row_stat[1, late]
        delta = row_stat[2, late]
        prob = weight_buf[tile] * level[:1]
        dscore = (prob * ((dprob_buf[tile] - delta[:1]) * score_scale)).astype(jnp.bfloat16)
        prob = prob.astype(jnp.bfloat16)
        keys_t = table_t[block]
        out_acc[late] += nn_dot(keys_t[:LAT], prob)
        dquery_acc[late] += nn_dot(keys_t, dscore)
        dkey_acc[block, :LAT] += nt_dot(query_t[late, :LAT], dscore) + nt_dot(grad_t[late], prob)
        dkey_acc[block, LAT:] += nt_dot(query_t[late, LAT:width], dscore)

    over_tiles(grad_tile)
    heads_in = chunk // half_rows
    for c in range(rows // chunk):
        span = slice(c * chunk, (c + 1) * chunk)
        outs, leads, tails = [], [], []
        for h in range(2):
            outs.append(nt_dot(eye[...], out_acc[h, :, span].astype(jnp.bfloat16)).astype(jnp.bfloat16))
            a = dquery_acc[h, LAT : LAT + half, span]
            b = dquery_acc[h, LAT + half :, span]
            cos, sin = (
                jnp.concatenate([ref[h, :half]] * (chunk // pair), axis=1) for ref in (cos_ref, sin_ref)
            )
            turned = jnp.concatenate(
                [dquery_acc[h, :LAT, span], a * cos + b * sin, b * cos - a * sin], axis=0
            ).astype(jnp.bfloat16)
            turned = nt_dot(eye[...], turned).astype(jnp.bfloat16)
            leads.append(turned[:, :LAT])
            tails.append(turned[:, LAT:])
        pieces = []
        for k in range(heads_in):
            n = c * heads_in + k
            part = slice(k * half_rows, (k + 1) * half_rows)
            both = lambda pair_of: jnp.concatenate([pair_of[0][part], pair_of[1][part]], axis=0)
            attended_ref[:, n * VDIM : (n + 1) * VDIM] = nn_dot(
                both(outs), value_up_ref[:, n * VDIM : (n + 1) * VDIM]
            ).astype(jnp.bfloat16)
            pieces.append(
                nn_dot(both(leads), key_up_ref[:, n * NOPE : (n + 1) * NOPE]).astype(jnp.bfloat16)
            )
            pieces.append(both(tails))
        grad_queries_ref[:, c * heads_in * head : (c + 1) * heads_in * head] = jnp.concatenate(
            pieces, axis=1
        )

    @pl.when(step == pl.num_programs(0) - 1)
    def _():
        per = key_block // quarter
        for j in range(blocks):
            turned = nt_dot(
                eye[:key_block, :key_block], dkey_acc[j].astype(jnp.bfloat16)
            ).astype(grad_keys_ref.dtype)
            for k in range(per):
                grad_keys_ref[pieces_of[j * per + k][1]] = turned[k * quarter : (k + 1) * quarter]


def attention(keys, queries, grad_out, key_up, value_up, cos_table, sin_table, groups):
    tokens = queries.shape[0]
    half_rows = tokens // 2
    head_count = key_up.shape[1] // NOPE
    group = group_size(head_count)
    key_total = tokens * groups
    key_block = 256
    blocks = key_total // key_block
    padded = LAT + 2 * ROPE
    width = LAT + ROPE
    rows = group * half_rows

    def turn(table):
        table = table.T.reshape(ROPE // 2, 2, half_rows).transpose(1, 0, 2)
        return jnp.tile(table, (1, 2, 2))

    cos_t, sin_t = turn(cos_table), turn(sin_table)
    body = functools.partial(
        attention_kernel, groups, group, key_block, (NOPE + ROPE) ** (-0.5)
    )
    whole = lambda shape: pl.BlockSpec(shape, lambda i: (0,) * len(shape), pipeline_mode=pl.Buffered(1))
    column = lambda height, width: pl.BlockSpec((height, group * width), lambda i: (0, i))
    return pl.pallas_call(
        body,
        grid=(head_count // group,),
        in_specs=[
            whole(keys.shape),
            column(tokens, NOPE + ROPE),
            column(tokens, VDIM),
            column(LAT, NOPE),
            column(LAT, VDIM),
            whole(cos_t.shape),
            whole(sin_t.shape),
        ],
        out_specs=[
            column(tokens, VDIM),
            column(tokens, NOPE + ROPE),
            whole(keys.shape),
        ],
        out_shape=[
            jax.ShapeDtypeStruct((tokens, head_count * VDIM), jnp.bfloat16),
            jax.ShapeDtypeStruct((tokens, head_count * (NOPE + ROPE)), jnp.bfloat16),
            jax.ShapeDtypeStruct(keys.shape, jnp.bfloat16),
        ],
        scratch_shapes=[
            pltpu.VMEM((key_total, padded), jnp.bfloat16),
            pltpu.VMEM((blocks, width, key_block), jnp.bfloat16),
            pltpu.VMEM((2, padded, rows), jnp.bfloat16),
            pltpu.VMEM((2, LAT, rows), jnp.bfloat16),
            pltpu.VMEM((blocks + 1, key_block, rows), jnp.float32),
            pltpu.VMEM((blocks + 1, key_block, rows), jnp.float32),
            pltpu.VMEM((blocks + 1, 8, rows), jnp.float32),
            pltpu.VMEM((2, LAT, rows), jnp.float32),
            pltpu.VMEM((2, width, rows), jnp.float32),
            pltpu.VMEM((blocks, width, key_block), jnp.float32),
            pltpu.VMEM((3, 2, 8, rows), jnp.float32),
            pltpu.VMEM((256, 256), jnp.bfloat16),
        ],
        compiler_params=pltpu.CompilerParams(
            dimension_semantics=("arbitrary",), vmem_limit_bytes=60 * 1024 * 1024
        ),
        name="attention",
    )(keys, queries, grad_out, key_up, value_up, cos_t, sin_t)


class Place:
    def __init__(self):
        index = lax.axis_index("ctx")
        self.core = index % 2
        self.x = (index // 2) % 2
        self.z = index // 4
        self.y = lax.axis_index("tp")
        self.depth = lax.axis_size("ctx") // 4

    def device(self, z=None, x=None, core=None, y=None):
        z = self.z if z is None else z
        x = self.x if x is None else x
        core = self.core if core is None else core
        y = self.y if y is None else y
        return ((z * 2 + x) * 2 + core, y)

    def partners(self):
        others = [
            self.device(z=(self.z + k) % self.depth) for k in range(1, self.depth)
        ]
        sides = [
            self.device(x=1 - self.x),
            self.device(y=1 - self.y),
            self.device(core=1 - self.core),
        ]
        return others, sides

    def greet(self):
        others, sides = self.partners()
        barrier = pltpu.get_barrier_semaphore()
        for device in others + sides:
            pl.semaphore_signal(
                barrier, inc=1, device_id=device, device_id_type=pl.DeviceIdType.MESH
            )
        pl.semaphore_wait(barrier, len(others + sides))


def sender(send_sem, recv_sem):
    def send(slot, source, target, device):
        copy = pltpu.make_async_remote_copy(
            src_ref=source,
            dst_ref=target,
            send_sem=send_sem.at[slot],
            recv_sem=recv_sem.at[slot],
            device_id=device,
            device_id_type=pl.DeviceIdType.MESH,
        )
        copy.start()
        return copy

    return send


def gather_kernel(own_ref, full_ref, send_sem, recv_sem):
    me = Place()
    c, x, y, z = me.core, me.x, me.y, me.z
    others, (across_x, across_y, sibling) = me.partners()
    me.greet()
    send = sender(send_sem, recv_sem)
    base = len(others)
    along = [
        send(k, own_ref, full_ref.at[:, c, y, x, z], device) for k, device in enumerate(others)
    ]
    full_ref[:, c, y, x, z] = own_ref[...]
    for copy in along:
        copy.wait_recv()
    line = full_ref.at[:, c, y, x]
    a2 = send(base, full_ref.at[0, c, y, x], full_ref.at[0, c, y, x], across_x)
    b2 = send(base + 1, full_ref.at[1, c, y, x], full_ref.at[1, c, y, x], across_y)
    c1 = send(base + 2, line, line, sibling)
    a2.wait_recv()
    a3 = send(base + 3, full_ref.at[0, c, y], full_ref.at[0, c, y], across_y)
    got = full_ref.at[0, c, y, 1 - x]
    c2 = send(base + 4, got, got, sibling)
    b2.wait_recv()
    b3 = send(base + 5, full_ref.at[1, c, :, x], full_ref.at[1, c, :, x], across_x)
    got = full_ref.at[1, c, 1 - y, x]
    c3 = send(base + 6, got, got, sibling)
    a3.wait_recv()
    got = full_ref.at[0, c, 1 - y]
    c4 = send(base + 7, got, got, sibling)
    b3.wait_recv()
    got = full_ref.at[1, c, :, 1 - x]
    c5 = send(base + 8, got, got, sibling)
    for copy in (c1, c2, c3, c4, c5):
        copy.wait_recv()
    for copy in along + [a2, b2, c1, a3, c2, b3, c3, c4, c5]:
        copy.wait_send()


def scatter_kernel(
    part_ref, out_ref, got1, sum1, got2, sum2, got3, sum3, got4, send_sem, recv_sem
):
    me = Place()
    c, x, y, z = me.core, me.x, me.y, me.z
    others, (across_x, across_y, sibling) = me.partners()
    me.greet()
    send = sender(send_sem, recv_sem)
    wide = lambda value: value.astype(jnp.float32)
    add = lambda a, b: (wide(a) + wide(b)).astype(jnp.bfloat16)
    base = len(others)
    s0 = send(base, part_ref.at[0, 1 - c, 1 - y], got1.at[0, 1 - y], sibling)
    s1 = send(base + 1, part_ref.at[1, 1 - c, :, 1 - x], got1.at[1, :, 1 - x], sibling)
    s2 = send(base + 2, part_ref.at[0, 1 - c, y], got1.at[0, y], sibling)
    s3 = send(base + 3, part_ref.at[1, 1 - c, :, x], got1.at[1, :, x], sibling)
    s0.wait_recv()
    sum1[0, 1 - y] = add(part_ref[0, c, 1 - y], got1[0, 1 - y])
    a2 = send(base + 4, sum1.at[0, 1 - y], got2.at[0], across_y)
    s1.wait_recv()
    sum1[1, :, 1 - x] = add(part_ref[1, c, :, 1 - x], got1[1, :, 1 - x])
    b2 = send(base + 5, sum1.at[1, :, 1 - x], got2.at[1], across_x)
    s2.wait_recv()
    sum1[0, y] = add(part_ref[0, c, y], got1[0, y])
    s3.wait_recv()
    sum1[1, :, x] = add(part_ref[1, c, :, x], got1[1, :, x])
    a2.wait_recv()
    sum2[0, 1 - x] = add(sum1[0, y, 1 - x], got2[0, 1 - x])
    a3 = send(base + 6, sum2.at[0, 1 - x], got3.at[0], across_x)
    b2.wait_recv()
    sum2[1, 1 - y] = add(sum1[1, 1 - y, x], got2[1, 1 - y])
    b3 = send(base + 7, sum2.at[1, 1 - y], got3.at[1], across_y)
    sum2[0, x] = add(sum1[0, y, x], got2[0, x])
    sum2[1, y] = add(sum1[1, y, x], got2[1, y])
    a3.wait_recv()
    sum3[0] = add(sum2[0, x], got3[0])
    b3.wait_recv()
    sum3[1] = add(sum2[1, y], got3[1])
    along = [
        send(k, sum3.at[:, (z + k + 1) % me.depth], got4.at[k], device)
        for k, device in enumerate(others)
    ]
    total = wide(sum3[:, z])
    for k, copy in enumerate(along):
        copy.wait_recv()
        total = total + wide(got4[k])
    out_ref[...] = total
    for copy in along + [s0, s1, s2, s3, a2, b2, a3, b3]:
        copy.wait_send()


def vmem_call(body, out_shape, scratch, identity, name):
    return pl.pallas_call(
        body,
        out_shape=out_shape,
        in_specs=[pl.BlockSpec(memory_space=pltpu.VMEM)],
        out_specs=pl.BlockSpec(memory_space=pltpu.VMEM),
        scratch_shapes=scratch,
        compiler_params=pltpu.CompilerParams(
            collective_id=identity, has_side_effects=True, vmem_limit_bytes=40 * 1024 * 1024
        ),
        name=name,
    )


def gather_keys(own):
    depth = lax.axis_size("ctx") // 4
    shape = (2, 2, 2, 2, depth) + own.shape[1:]
    sems = pltpu.SemaphoreType.DMA((depth + 8,))
    return vmem_call(
        gather_kernel, jax.ShapeDtypeStruct(shape, own.dtype), [sems, sems], 0, "gather_keys"
    )(own)


def scatter_keys(parts):
    depth = parts.shape[4]
    block = parts.shape[5:]
    sems = pltpu.SemaphoreType.DMA((depth + 7,))
    buffer = lambda *lead: pltpu.VMEM(lead + block, parts.dtype)
    scratch = [
        buffer(2, 2, 2, depth),
        buffer(2, 2, 2, depth),
        buffer(2, 2, depth),
        buffer(2, 2, depth),
        buffer(2, depth),
        buffer(2, depth),
        buffer(depth - 1, 2),
        sems,
        sems,
    ]
    return vmem_call(
        scatter_kernel,
        jax.ShapeDtypeStruct((2,) + block, jnp.float32),
        scratch,
        1,
        "scatter_keys",
    )(parts)


SWAP = [(0, 1), (1, 0)]


def on_device(
    hidden,
    embed,
    gain_hidden,
    gain_embed,
    proj_hidden,
    proj_embed,
    gain_latent,
    key_up,
    value_up,
    queries,
    grad_out,
):
    tokens = hidden.shape[0]
    half_rows = tokens // 2
    groups = lax.axis_size("ctx")
    ctx_index = lax.axis_index("ctx")
    edge_rows = jnp.stack([embed[0], embed[half_rows]], axis=0)
    padded = with_halo(edge_rows, (("ctx", 0),), 1)
    after_early = jnp.where(ctx_index == groups - 1, embed[half_rows], padded[3])
    next_embed = jnp.concatenate(
        [embed[1:half_rows], after_early[None], embed[half_rows + 1 :], padded[0][None]], axis=0
    )
    hidden_wide = hidden.astype(jnp.float32)
    next_wide = next_embed.astype(jnp.float32)
    squares = jnp.stack(
        [jnp.sum(hidden_wide * hidden_wide, axis=1), jnp.sum(next_wide * next_wide, axis=1)], axis=1
    )
    scaled_hidden = (hidden_wide * gain_hidden).astype(jnp.bfloat16)
    scaled_next = (next_wide * gain_embed).astype(jnp.bfloat16)
    part_hidden = jnp.dot(scaled_hidden, proj_hidden, preferred_element_type=jnp.float32)
    part_next = jnp.dot(scaled_next, proj_embed, preferred_element_type=jnp.float32)
    positions = local_positions(tokens, ctx_index, groups)
    cos_table, sin_table = rotation(positions)
    paired = lax.axis_size("tp") == 2
    depth = groups // 4
    quarter = half_rows // 2
    if paired:
        tp_index = lax.axis_index("tp")
        half_of = lambda value, k: lax.dynamic_slice_in_dim(value, k * half_rows, half_rows, 0)
        part_hidden, part_next, squares = (
            half_of(v, tp_index) + lax.ppermute(half_of(v, 1 - tp_index), "tp", SWAP)
            for v in (part_hidden, part_next, squares)
        )
        positions = half_of(positions, tp_index)
    else:
        part_hidden, part_next, squares = lax.psum((part_hidden, part_next, squares), "tp")
    key_latent, key_rope, latent, inverse, inv_latent = finish_latent(
        part_hidden, part_next, squares, gain_latent, positions
    )
    keys = jnp.concatenate([key_latent, key_rope], axis=1)
    if paired:
        keys = gather_keys(keys.reshape(2, quarter, LAT + ROPE))
    else:
        keys = lax.all_gather(keys, "ctx", axis=0, tiled=True)
        keys = keys.reshape(depth, 2, 2, 2, 2, quarter, LAT + ROPE)
        keys = keys.transpose(4, 2, 3, 1, 0, 5, 6)
    attended, grad_queries, grad_keys = attention(
        keys,
        queries,
        grad_out,
        key_up,
        value_up,
        cos_table,
        sin_table,
        groups,
    )
    if paired:
        grad_keys = scatter_keys(grad_keys).reshape(half_rows, LAT + ROPE)
    else:
        grad_keys = grad_keys.transpose(4, 3, 1, 2, 0, 5, 6).reshape(-1, LAT + ROPE)
        grad_keys = lax.psum_scatter(grad_keys, "ctx", scatter_dimension=0, tiled=True)
        grad_keys = lax.psum(grad_keys.astype(jnp.float32), "tp")
    grad_key_latent, grad_key_rope = grad_keys[:, :LAT], grad_keys[:, LAT:]
    part_grad_hidden, part_grad_next, coefficient = latent_backward(
        grad_key_latent,
        grad_key_rope,
        latent,
        inverse,
        inv_latent,
        gain_latent,
        positions,
        part_hidden,
        part_next,
    )
    if paired:

        def both_halves(value):
            other = lax.ppermute(value, "tp", SWAP)
            early = jnp.where(tp_index == 0, value, other)
            late = jnp.where(tp_index == 0, other, value)
            return jnp.concatenate([early, late], axis=0)

        part_grad_hidden = both_halves(part_grad_hidden)
        part_grad_next = both_halves(part_grad_next)
        coefficient = both_halves(coefficient)
    grad_hidden = (
        gain_hidden
        * jnp.einsum("rc,dc->rd", part_grad_hidden, proj_hidden, preferred_element_type=jnp.float32)
        - coefficient[:, 0:1] * hidden_wide
    ).astype(jnp.bfloat16)
    grad_next = (
        gain_embed
        * jnp.einsum("rc,dc->rd", part_grad_next, proj_embed, preferred_element_type=jnp.float32)
        - coefficient[:, 1:2] * next_wide
    )
    grad_next_rounded = grad_next.astype(jnp.bfloat16)
    edge_grads = jnp.stack(
        [grad_next_rounded[tokens - 1], grad_next_rounded[half_rows - 1]], axis=0
    )
    returned = with_halo(edge_grads, (("ctx", 0),), 1)
    before_late = jnp.where(ctx_index == groups - 1, grad_next_rounded[half_rows - 1], returned[3])
    grad_embed = jnp.concatenate(
        [
            returned[0][None],
            grad_next_rounded[: half_rows - 1],
            before_late[None],
            grad_next_rounded[half_rows : tokens - 1],
        ],
        axis=0,
    )
    return (attended, grad_queries, grad_hidden, grad_embed)


def solution(mesh):
    placed = (
        P("ctx", "tp"),
        P("ctx", "tp"),
        P("tp"),
        P("tp"),
        P("tp", None),
        P("tp", None),
        P(),
        P(None, "tp"),
        P(None, "tp"),
        P("ctx", "tp"),
        P("ctx", "tp"),
    )
    return jax.shard_map(
        on_device,
        mesh=mesh,
        in_specs=placed,
        out_specs=(P("ctx", "tp"), P("ctx", "tp"), P("ctx", "tp"), P("ctx", "tp")),
        check_vma=False,
    )
```
